32 devices in a mesh: band: 4 (over z), strip: 8 (over y, x, core).
Axes of the slice: x: 2, y: 2, z: 4, core: 2. Of those that a mesh axis runs over, the one named last changes fastest.
Arguments:
- first_scene: bfloat16 [2048, 4096], P('band', 'strip'), may hold values from -6 to 6
- second_scene: bfloat16 [2048, 4096], P('band', 'strip'), may hold values from -6 to 6
- owner_strip: int32 [4, 8, 16, 1], P('band', 'strip'), may hold values from 0 to 7; in each aligned block of 16 rows (0 to 15, 16 to 31, ..., all dimensions but the last counted through in order) at most 4 rows name the same one
- target_tile: int32 [4, 8, 16], P('band', 'strip'), may hold values from 0 to 15
- offsets: int32 [4, 8, 16, 2], P('band', 'strip'), may hold values from -32 to 32
- valid_mask: int32 [4, 8, 16], P('band', 'strip'), may hold values 0 or 1
Outputs:
- consistency: float32 [4, 8, 16, 4096], P('band', 'strip')
The draws below stay inside these ranges and needn't reach their ends.
Inputs may be any that keep to these rules, and one draw needn't show every extreme that they name: `owner_strip`: among the 16 patches of one device at most 4 name the same owner strip, and in every draw some device has 4 patches naming one strip.
All inputs are finite; a program needn't handle non-finite values. No bound on the sum of `valid_mask` on one device may be relied on, other than what follows from the above.
Results may differ from the reference program's by a relative error of at most 0.0003.
Values may be sent and summed in bfloat16 or wider, within the bound.
A program may use at most 128 MiB of HBM per device.

```python
import math
import jax
import jax.numpy as jnp
import numpy as np
from jax import lax

PATCH_SIDE = 128
SHIFTS = 64
ROW_PATCHES = 4
COL_PATCHES = 4
PATCHES = 16
SEARCH = 192
PADDED = 256
CAPACITY = 4
IMAGE_ROWS = 2048
IMAGE_COLS = 4096
N_BAND = 4
N_STRIP = 8


def place_ends(result, own_key, least, top_value):
    dims = result.shape
    spot = [jax.random.randint(jax.random.fold_in(own_key, axis), (), 0, dims[axis]) for axis in range(len(dims))]
    result = result.at[tuple(spot)].set(least)
    longest = dims.index(max(dims))
    spot[longest] = (spot[longest] + 1) % dims[longest]
    return result.at[tuple(spot)].set(top_value)


def block_scale(key, extent, pieces, low, high):
    def one(position, shards_of):
        steps = jax.random.uniform(jax.random.fold_in(jax.random.fold_in(key, 6), position), (shards_of,), jnp.float32, low / len(pieces), high / len(pieces))
        return jnp.repeat(jnp.exp(steps), extent[position] // shards_of).reshape((-1,) + (1,) * (len(extent) - position - 1))

    level = one(*pieces[0])
    for cut in pieces[1:]:
        level = level * one(*cut)
    return level


def assign_block(key, own, number, rows, number_of, top, limit, lean):
    sequence = jax.random.permutation(key, number_of)
    packed, usual = portions_of(number_of, rows * top, limit, lean, True), portions_of(number_of, rows * top, limit, lean, False)
    places = jnp.arange(number_of)

    def named(tallies, turn):
        used = int((tallies > 0).sum())
        fixed = max(1, used // 4)
        passed = fixed + (places - fixed + turn * (used - fixed)) % max(1, number_of - fixed)
        return jnp.zeros((number_of,), jnp.int32).at[sequence[jnp.where(places < fixed, places, passed)]].set(jnp.asarray(tallies, jnp.int32))

    tallies = jnp.where(number % 4 == 0, named(packed, number // 4), named(usual, number - number // 4 - 1))
    mixed = jax.random.permutation(jax.random.fold_in(own, 3), number_of)
    giver, receiver = mixed[0:number_of // 2 * 2:2], mixed[1:number_of // 2 * 2:2]
    margin = jnp.minimum(tallies[giver] - 1, limit - tallies[receiver]) // 2
    margin = jnp.where((giver == sequence[0]) | (receiver == sequence[0]) | (tallies[receiver] == 0), 0, jnp.maximum(margin, 0))
    passed = jax.random.randint(jax.random.fold_in(own, 4), (number_of // 2,), 0, 1 << 20) % (margin + 1)
    tallies = tallies.at[giver].add(-passed).at[receiver].add(passed)
    labels = jnp.searchsorted(jnp.cumsum(tallies), jnp.arange(rows * top), side="right").astype(jnp.int32)
    listing = labels.reshape(top, rows).T
    listing = listing[jax.random.permutation(jax.random.fold_in(own, 1), rows)]
    turn = jax.random.randint(jax.random.fold_in(own, 2), (rows, 1), 0, top)
    return jnp.take_along_axis(listing, (jnp.arange(top)[None, :] + turn) % top, axis=1)


def portions_of(number_of, total, bound, slope, full):
    weights = [(1 << 20) // math.isqrt(standing ** slope) + 1 for standing in range(1, number_of + 1)]
    largest = bound if full else min(bound, max(-(-total // number_of), total * weights[0] // sum(weights)))
    least = 1 if total - largest >= number_of - 1 else 0
    given, spare = [largest] + [least] * (number_of - 1), total - largest - least * (number_of - 1)
    while spare > 0:
        movable = [i for i in range(1, number_of) if given[i] < largest] or [i for i in range(1, number_of) if given[i] < bound]
        whole, remaining = sum([weights[i] for i in movable]), spare
        for i in movable:
            more = min(bound - given[i], max(1, remaining * weights[i] // whole), spare)
            given[i] = given[i] + more
            spare = spare - more
    return np.array(given)


def noise(key, shape, spread, bound, pieces=(), held_as=jnp.bfloat16):
    gain = block_scale(key, shape, pieces, -0.22, 0.18) if pieces else 1.0
    values = jax.random.normal(key, shape, jnp.float32) * spread * gain
    return jnp.minimum(jnp.maximum(values, -bound), bound).astype(held_as)


def setup_inputs(seed: int = 0) -> dict:
    key_list = jax.random.split(jax.random.key(seed), 7)
    first_scene = noise(key_list[0], (IMAGE_ROWS, IMAGE_COLS), 1.0, 6.0, ((0, 4), (1, 8)))
    second_scene = noise(key_list[1], (IMAGE_ROWS, IMAGE_COLS), 1.0, 6.0, ((0, 4), (1, 8)))
    owner_strip_keys = jax.random.split(jax.random.fold_in(key_list[2], 1), N_BAND * N_STRIP * PATCHES // PATCHES)
    owner_strip_turns = jax.random.permutation(jax.random.fold_in(key_list[2], 3), N_BAND * N_STRIP * PATCHES // PATCHES)
    owner_strip = jax.vmap(lambda own, number: assign_block(jax.random.fold_in(key_list[2], 2), own, number, PATCHES, N_STRIP, 1, CAPACITY, 2))(owner_strip_keys, owner_strip_turns).reshape((N_BAND, N_STRIP, PATCHES, 1))
    target_tile = place_ends(jax.random.randint(key_list[3], (N_BAND, N_STRIP, PATCHES), 0, PATCHES), jax.random.fold_in(key_list[3], 1), 0, PATCHES - 1).astype(jnp.int32)
    offsets = place_ends(jax.random.randint(key_list[4], (N_BAND, N_STRIP, PATCHES, 2), 0 - SHIFTS // 2, SHIFTS // 2 + 1), jax.random.fold_in(key_list[4], 1), 0 - SHIFTS // 2, (SHIFTS // 2 + 1) - 1).astype(jnp.int32)
    valid_mask = place_ends((jax.random.randint(key_list[5], (N_BAND, N_STRIP, PATCHES), 0, 4) < 3).astype(jnp.int32), jax.random.fold_in(key_list[5], 1), 0, 1)
    return dict(first_scene=first_scene, second_scene=second_scene, owner_strip=owner_strip, target_tile=target_tile, offsets=offsets, valid_mask=valid_mask)


EPSILON = 1e-05

def normalize(patch):
    centered = patch - jnp.mean(patch)
    return centered * lax.rsqrt(jnp.mean(centered * centered) + EPSILON)

def correlate(template, window):
    spec_template = jnp.fft.rfft2(template, s=(PADDED, PADDED))
    spec_window = jnp.fft.rfft2(window, s=(PADDED, PADDED))
    surface = jnp.fft.irfft2(jnp.conj(spec_template) * spec_window, s=(PADDED, PADDED))
    return surface[:SHIFTS, :SHIFTS]

def reference(first_scene, second_scene, owner_strip, target_tile, offsets, valid_mask):
    middle = SHIFTS // 2
    padded_first = jnp.pad(first_scene, SHIFTS)
    padded_second = jnp.pad(second_scene, SHIFTS)
    patch_total = N_BAND * N_STRIP * PATCHES
    owners = owner_strip.reshape(patch_total).astype(jnp.int32)
    tile_list = target_tile.reshape(patch_total).astype(jnp.int32)
    shifts = offsets.reshape(patch_total, 2).astype(jnp.int32)
    mask_list = valid_mask.reshape(patch_total)
    indices = jnp.arange(patch_total, dtype=jnp.int32)

    def one_patch(inputs):
        patch_index, strip_owner, tile_index, fine_shift, keep_flag = inputs
        band_index = patch_index // (N_STRIP * PATCHES)
        strip_index = patch_index // PATCHES % N_STRIP
        local_index = patch_index % PATCHES
        patch_top = (band_index * ROW_PATCHES + local_index // COL_PATCHES) * PATCH_SIDE
        patch_left = (strip_index * COL_PATCHES + local_index % COL_PATCHES) * PATCH_SIDE
        target_top = (band_index * ROW_PATCHES + tile_index // COL_PATCHES) * PATCH_SIDE
        target_left = (strip_owner * COL_PATCHES + tile_index % COL_PATCHES) * PATCH_SIDE
        search = lax.dynamic_slice(padded_second, ((target_top + fine_shift[0] - middle + SHIFTS).astype(jnp.int32), (target_left + fine_shift[1] - middle + SHIFTS).astype(jnp.int32)), (SEARCH, SEARCH)).astype(jnp.float32)
        beside_all = lax.dynamic_slice(padded_first, ((patch_top - middle + 1 + SHIFTS).astype(jnp.int32), (patch_left - middle + 1 + SHIFTS).astype(jnp.int32)), (SEARCH, SEARCH)).astype(jnp.float32)
        template = normalize(beside_all[middle - 1:middle - 1 + PATCH_SIDE, middle - 1:middle - 1 + PATCH_SIDE])
        backward = normalize(search[middle:middle + PATCH_SIDE, middle:middle + PATCH_SIDE])
        forward_surface = correlate(template, search)
        backward_surface = correlate(backward, beside_all)
        combined = (forward_surface + backward_surface[::-1, ::-1]) / (2.0 * PATCH_SIDE)
        return (combined * keep_flag.astype(jnp.float32)).reshape(SHIFTS * SHIFTS)
    surfaces = lax.map(one_patch, (indices, owners, tile_list, shifts, mask_list))
    return surfaces.reshape(N_BAND, N_STRIP, PATCHES, SHIFTS * SHIFTS)
```

```python
import functools

import jax
import jax.numpy as jnp
import numpy as np
from jax import lax
from jax.experimental import pallas as pl
from jax.experimental.pallas import tpu as pltpu
from jax.sharding import PartitionSpec as P

PATCH_SIDE = 128
SHIFTS = 64
EDGE = SHIFTS // 2
SEARCH = PATCH_SIDE + SHIFTS
CYCLE = SEARCH - 1
BINS = (CYCLE + 1) // 2
LANES = 128
WIDE = 2 * LANES
HALO = 64
ROWS = SEARCH + 16
EPSILON = 1e-05
F32 = jnp.float32
BF16 = jnp.bfloat16


def two(x):
    high = x.astype(BF16)
    return high, (x - high.astype(F32)).astype(BF16)


def two_np(x):
    high = x.astype(jnp.bfloat16)
    low = (x - high.astype(np.float64)).astype(jnp.bfloat16)
    return high, low


def tables():
    angle = 2 * np.pi / CYCLE
    freq = np.arange(BINS)

    def across(place, real):
        out = np.zeros((LANES, WIDE))
        phase = angle * place[:, None] * freq[None, :]
        out[:, :BINS] = np.cos(phase) * real[:, None]
        out[:, LANES : LANES + BINS] = np.sin(phase) * real[:, None]
        return out

    def down(place, real):
        phase = angle * place[None, :] * freq[:, None]
        return np.concatenate([np.cos(phase), np.sin(phase)], axis=0) * real[None, :]

    lane = np.arange(LANES)
    edge_place = np.where(lane < LANES // 2, PATCH_SIDE + lane, lane - LANES)
    row = np.arange(SEARCH) - EDGE
    made = {}
    sums = []
    inner = across(lane, np.ones(LANES))
    high, low = two_np(inner)
    made["inner"] = np.concatenate([high, low], axis=0)
    sums.append((high.astype(np.float64) + low.astype(np.float64)).sum(0))
    high, low = two_np(down(row[EDGE : EDGE + PATCH_SIDE], np.ones(PATCH_SIDE)))
    made["down_inner"] = np.concatenate([high, high, low], axis=1)
    for name, first, last in (("search", -EDGE, CYCLE - EDGE), ("around", 1 - EDGE, CYCLE - EDGE + 1)):
        real = (edge_place >= first) & (edge_place < last)
        real &= (lane < EDGE) | (lane >= LANES - EDGE)
        high, low = two_np(across(edge_place, real))
        made["edge_" + name] = np.concatenate([high, low], axis=0)
        sums.append(sums[0] + (high.astype(np.float64) + low.astype(np.float64)).sum(0))
        high, low = two_np(down(row, (row >= first) & (row < last)))
        made["down_" + name] = np.concatenate([high, high, low], axis=1)
    made["sums"] = np.concatenate([np.stack(sums), np.zeros((5, WIDE))], axis=0).astype(np.float32)
    lag = np.concatenate([np.arange(0, SHIFTS, 2), np.arange(1, SHIFTS, 2)]) - EDGE
    weight = np.where(freq == 0, 1.0, 2.0)
    phase = angle * lag[:, None] * freq[None, :]
    back = np.concatenate([np.cos(phase) * weight, np.sin(phase) * weight], axis=1)
    high, low = two_np(back)
    made["back_down"] = np.concatenate([high, high, low], axis=1)
    lag = np.arange(LANES) % SHIFTS - EDGE
    phase = angle * freq[:, None] * lag[None, :]
    back = np.zeros((WIDE, LANES))
    back[:BINS] = np.cos(phase) * weight[:, None]
    back[LANES : LANES + BINS] = np.sin(phase) * weight[:, None]
    high, low = two_np(back)
    made["back_across"] = np.concatenate([high, high, low], axis=0)
    return made


NAMES = (
    "inner",
    "edge_search",
    "edge_around",
    "down_inner",
    "down_search",
    "down_around",
    "back_down",
    "back_across",
    "sums",
)


def dot(a, b):
    return jnp.dot(a, b, preferred_element_type=F32)


def thrice(x):
    high, low = two(x)
    return jnp.concatenate([high, low, high], axis=0)


def statistics(patch):
    count = PATCH_SIDE * PATCH_SIDE
    mean = jnp.sum(patch) / count
    centered = patch - mean
    return mean, lax.rsqrt(jnp.full((1, LANES), jnp.sum(centered * centered) / count + EPSILON))


def spectra(inner, edge, mean, table, name, row):
    core = dot(jnp.concatenate([inner, inner], axis=1), table["inner"][...])
    rim = dot(jnp.concatenate([edge, edge], axis=1), table["edge_" + name][...])
    sums = table["sums"]
    full = core + rim - mean * sums[row : row + 1, :]
    core = core[EDGE : EDGE + PATCH_SIDE] - mean * sums[0:1, :]
    return dot(table["down_" + name][...], thrice(full)), dot(table["down_inner"][...], thrice(core))


def quarters(x):
    return x[:BINS, :LANES], x[BINS:, :LANES], x[:BINS, LANES:], x[BINS:, LANES:]


def matched(x, y):
    x0, x1, x2, x3 = quarters(x)
    y0, y1, y2, y3 = quarters(y)
    return (
        x0 * y0 + x1 * y1 + x2 * y2 + x3 * y3,
        x1 * y0 - x0 * y1 + x3 * y2 - x2 * y3,
        x2 * y0 - x0 * y2 + x3 * y1 - x1 * y3,
        x0 * y3 + x3 * y0 - x1 * y2 - x2 * y1,
    )


def kernel(owner, tile, offset, valid, first, second, *refs):
    table = dict(zip(NAMES, refs[: len(NAMES)]))
    out_ref, middle_ref, side_ref = refs[len(NAMES) :]
    patch_count = out_ref.shape[0]
    per_row = second.shape[2] // LANES
    tiles = second.shape[0] * per_row
    lane = lax.broadcasted_iota(jnp.int32, (1, LANES), 1)
    halves = lane < LANES // 2

    def one(k, carry):
        top = pl.multiple_of(k // per_row * PATCH_SIDE + HALO - EDGE, 16)
        rows = pl.ds(top, SEARCH)

        def place_of(c):
            return pl.ds(pl.multiple_of(c * LANES, LANES), LANES)

        here = k % per_row
        inner_a = first[rows, place_of(here + 1)]
        edge_a = jnp.where(halves, first[rows, place_of(here + 2)], first[rows, place_of(here)])
        mean_a, gain_a = statistics(inner_a[EDGE : EDGE + PATCH_SIDE].astype(F32))

        place = owner[k] * per_row + tile[k] % per_row
        row = tile[k] // per_row * PATCH_SIDE + HALO - EDGE + offset[2 * k]
        base = jnp.minimum(row // 16 * 16, second.shape[1] - ROWS)
        rows = pl.ds(pl.multiple_of(base, 16), ROWS)

        def block(c):
            c = jnp.clip(c, 0, tiles - 1)
            return second[c // per_row, rows, place_of(c % per_row)].astype(F32)

        right_end = jnp.where(place == tiles - 1, 0, LANES // 2)
        left_start = jnp.where(place == 0, LANES, LANES // 2)
        middle_ref[...] = block(place)
        side_ref[...] = jnp.where(
            lane < right_end, block(place + 1), jnp.where(lane >= left_start, block(place - 1), 0.0)
        )
        rows = pl.ds(row - base, SEARCH)
        dx = offset[2 * k + 1]
        turn = jnp.where(dx > 0, LANES - dx, -dx)
        middle = pltpu.roll(middle_ref[rows, :], turn, 1)
        side = pltpu.roll(side_ref[rows, :], turn, 1)
        within = (lane + dx >= 0) & (lane + dx < LANES)
        inner_s = jnp.where(within, middle, side)
        edge_s = jnp.where(within, side, middle).astype(BF16)
        mean_s, gain_s = statistics(inner_s[EDGE : EDGE + PATCH_SIDE])
        inner_s = inner_s.astype(BF16)

        around, around_inner = spectra(inner_a, edge_a, mean_a, table, "around", 2)
        search, search_inner = spectra(inner_s, edge_s, mean_s, table, "search", 1)
        scale = valid[k].astype(F32) / (2.0 * PATCH_SIDE * CYCLE * CYCLE)
        gain_a, gain_s = gain_a * scale, gain_s * scale
        a, b, c, d = [
            gain_a * ahead + gain_s * behind
            for ahead, behind in zip(matched(search, around_inner), matched(search_inner, around))
        ]
        spectrum = jnp.concatenate(
            [jnp.concatenate([a, c], axis=1), jnp.concatenate([b, d], axis=1)], axis=0
        )
        lines = dot(table["back_down"][...], thrice(spectrum))
        high, low = two(lines)
        surface = dot(jnp.concatenate([high, low, high], axis=1), table["back_across"][...])
        half = SHIFTS // 2
        out_ref[k] = jnp.where(halves, surface[:half], surface[half:])
        return carry

    lax.fori_loop(0, patch_count, one, 0)


def surfaces(first, gathered, owner, tile, offset, valid):
    patch_count = owner.shape[0]
    made = tables()
    return pl.pallas_call(
        kernel,
        out_shape=jax.ShapeDtypeStruct((patch_count, SHIFTS // 2, 2 * SHIFTS), F32),
        in_specs=[pl.BlockSpec(memory_space=pltpu.SMEM)] * 4
        + [pl.BlockSpec(memory_space=pltpu.VMEM)] * (2 + len(NAMES)),
        out_specs=pl.BlockSpec(memory_space=pltpu.VMEM),
        scratch_shapes=[pltpu.VMEM((ROWS, LANES), F32)] * 2,
    )(owner, tile, offset, valid, first, gathered, *[jnp.asarray(made[n]) for n in NAMES])


def both_ways(axis, tail, head):
    count = lax.axis_size(axis)
    before = lax.ppermute(tail, axis, [(i, i + 1) for i in range(count - 1)])
    after = lax.ppermute(head, axis, [(i + 1, i) for i in range(count - 1)])
    return before, after


def on_device(first_scene, second_scene, owner_strip, target_tile, offsets, valid_mask):
    per_row = first_scene.shape[1] // PATCH_SIDE
    patch_count = first_scene.shape[0] // PATCH_SIDE * per_row
    above, below = both_ways(
        "band",
        jnp.concatenate([first_scene[-HALO:], second_scene[-HALO:]], axis=0),
        jnp.concatenate([first_scene[:HALO], second_scene[:HALO]], axis=0),
    )
    second = jnp.concatenate([above[HALO:], second_scene, below[HALO:]], axis=0)
    gathered = lax.all_gather(second, "strip", axis=0)
    first = jnp.concatenate([above[:HALO], first_scene, below[:HALO]], axis=0)
    before, after = both_ways("strip", first[:, -LANES:], first[:, :LANES])
    first = jnp.concatenate([before, first, after], axis=1)
    result = surfaces(
        first,
        gathered,
        owner_strip.reshape(patch_count),
        target_tile.reshape(patch_count),
        offsets.reshape(2 * patch_count),
        valid_mask.reshape(patch_count),
    )
    return result.reshape(1, 1, patch_count, SHIFTS * SHIFTS)


def solution(mesh):
    return jax.shard_map(
        on_device,
        mesh=mesh,
        in_specs=(
            P("band", "strip"),
            P("band", "strip"),
            P("band", "strip", None, None),
            P("band", "strip", None),
            P("band", "strip", None, None),
            P("band", "strip", None),
        ),
        out_specs=P("band", "strip", None, None),
        check_vma=False,
    )
```

```python
import functools

import jax
import jax.numpy as jnp
import numpy as np
from jax import lax
from jax.experimental import pallas as pl
from jax.experimental.pallas import tpu as pltpu
from jax.sharding import PartitionSpec as P

PATCH_SIDE = 128
SHIFTS = 64
EDGE = SHIFTS // 2
SEARCH = PATCH_SIDE + SHIFTS
CYCLE = SEARCH - 1
BINS = (CYCLE + 1) // 2
LANES = 128
WIDE = 2 * LANES
HALO = 64
ROWS = SEARCH + 16
EPSILON = 1e-05
F32 = jnp.float32
BF16 = jnp.bfloat16


def two(x):
    high = x.astype(BF16)
    return high, (x - high.astype(F32)).astype(BF16)


def two_np(x):
    high = x.astype(jnp.bfloat16)
    low = (x - high.astype(np.float64)).astype(jnp.bfloat16)
    return high, low


def tables():
    angle = 2 * np.pi / CYCLE
    freq = np.arange(BINS)

    def across(place, real):
        out = np.zeros((LANES, WIDE))
        phase = angle * place[:, None] * freq[None, :]
        out[:, :BINS] = np.cos(phase) * real[:, None]
        out[:, LANES : LANES + BINS] = np.sin(phase) * real[:, None]
        return out

    def down(place, real):
        phase = angle * place[None, :] * freq[:, None]
        return np.concatenate([np.cos(phase), np.sin(phase)], axis=0) * real[None, :]

    lane = np.arange(LANES)
    edge_place = np.where(lane < LANES // 2, PATCH_SIDE + lane, lane - LANES)
    row = np.arange(SEARCH) - EDGE
    made = {}
    sums = []
    inner = across(lane, np.ones(LANES))
    high, low = two_np(inner)
    made["inner"] = np.concatenate([high, low], axis=0)
    sums.append((high.astype(np.float64) + low.astype(np.float64)).sum(0))
    high, low = two_np(down(row[EDGE : EDGE + PATCH_SIDE], np.ones(PATCH_SIDE)))
    made["down_inner"] = np.concatenate([high, high, low], axis=1)
    for name, first, last in (("search", -EDGE, CYCLE - EDGE), ("around", 1 - EDGE, CYCLE - EDGE + 1)):
        real = (edge_place >= first) & (edge_place < last)
        real &= (lane < EDGE) | (lane >= LANES - EDGE)
        high, low = two_np(across(edge_place, real))
        made["edge_" + name] = np.concatenate([high, low], axis=0)
        sums.append(sums[0] + (high.astype(np.float64) + low.astype(np.float64)).sum(0))
        high, low = two_np(down(row, (row >= first) & (row < last)))
        made["down_" + name] = np.concatenate([high, high, low], axis=1)
    made["sums"] = np.concatenate([np.stack(sums), np.zeros((5, WIDE))], axis=0).astype(np.float32)
    lag = np.concatenate([np.arange(0, SHIFTS, 2), np.arange(1, SHIFTS, 2)]) - EDGE
    weight = np.where(freq == 0, 1.0, 2.0)
    phase = angle * lag[:, None] * freq[None, :]
    back = np.concatenate([np.cos(phase) * weight, np.sin(phase) * weight], axis=1)
    high, low = two_np(back)
    made["back_down"] = np.concatenate([high, high, low], axis=1)
    lag = np.arange(LANES) % SHIFTS - EDGE
    phase = angle * freq[:, None] * lag[None, :]
    back = np.zeros((WIDE, LANES))
    back[:BINS] = np.cos(phase) * weight[:, None]
    back[LANES : LANES + BINS] = np.sin(phase) * weight[:, None]
    high, low = two_np(back)
    made["back_across"] = np.concatenate([high, high, low], axis=0)
    return made


NAMES = (
    "inner",
    "edge_search",
    "edge_around",
    "down_inner",
    "down_search",
    "down_around",
    "back_down",
    "back_across",
    "sums",
)


def dot(a, b):
    return jnp.dot(a, b, preferred_element_type=F32)


def thrice(x):
    high, low = two(x)
    return jnp.concatenate([high, low, high], axis=0)


def statistics(patch):
    count = PATCH_SIDE * PATCH_SIDE
    mean = jnp.sum(patch) / count
    centered = patch - mean
    return mean, lax.rsqrt(jnp.full((1, LANES), jnp.sum(centered * centered) / count + EPSILON))


def spectra(inner, edge, mean, table, name, row):
    core = dot(jnp.concatenate([inner, inner], axis=1), table["inner"][...])
    rim = dot(jnp.concatenate([edge, edge], axis=1), table["edge_" + name][...])
    sums = table["sums"]
    full = core + rim - mean * sums[row : row + 1, :]
    core = core[EDGE : EDGE + PATCH_SIDE] - mean * sums[0:1, :]
    return dot(table["down_" + name][...], thrice(full)), dot(table["down_inner"][...], thrice(core))


def quarters(x):
    return x[:BINS, :LANES], x[BINS:, :LANES], x[:BINS, LANES:], x[BINS:, LANES:]


def matched(x, y):
    x0, x1, x2, x3 = quarters(x)
    y0, y1, y2, y3 = quarters(y)
    return (
        x0 * y0 + x1 * y1 + x2 * y2 + x3 * y3,
        x1 * y0 - x0 * y1 + x3 * y2 - x2 * y3,
        x2 * y0 - x0 * y2 + x3 * y1 - x1 * y3,
        x0 * y3 + x3 * y0 - x1 * y2 - x2 * y1,
    )


def kernel(owner, tile, offset, valid, first, second, *refs):
    table = dict(zip(NAMES, refs[: len(NAMES)]))
    out_ref, middle_ref, side_ref = refs[len(NAMES) :]
    patch_count = out_ref.shape[0]
    per_row = second.shape[2] // LANES
    tiles = second.shape[0] * per_row
    lane = lax.broadcasted_iota(jnp.int32, (1, LANES), 1)
    halves = lane < LANES // 2

    def one(k, carry):
        top = pl.multiple_of(k // per_row * PATCH_SIDE, 16)
        rows = pl.ds(top, SEARCH)

        def place_of(c):
            return pl.ds(pl.multiple_of(c * LANES, LANES), LANES)

        here = k % per_row
        inner_a = first[rows, place_of(here + 1)]
        edge_a = jnp.where(halves, first[rows, place_of(here + 2)], first[rows, place_of(here)])
        mean_a, gain_a = statistics(inner_a[EDGE : EDGE + PATCH_SIDE].astype(F32))

        place = owner[k] * per_row + tile[k] % per_row
        row = tile[k] // per_row * PATCH_SIDE + HALO - EDGE + offset[2 * k]
        base = jnp.minimum(row // 16 * 16, second.shape[1] - ROWS)
        rows = pl.ds(pl.multiple_of(base, 16), ROWS)

        def block(c):
            c = jnp.clip(c, 0, tiles - 1)
            return second[c // per_row, rows, place_of(c % per_row)].astype(F32)

        right_end = jnp.where(place == tiles - 1, 0, LANES // 2)
        left_start = jnp.where(place == 0, LANES, LANES // 2)
        middle_ref[...] = block(place)
        side_ref[...] = jnp.where(
            lane < right_end, block(place + 1), jnp.where(lane >= left_start, block(place - 1), 0.0)
        )
        rows = pl.ds(row - base, SEARCH)
        dx = offset[2 * k + 1]
        turn = jnp.where(dx > 0, LANES - dx, -dx)
        middle = pltpu.roll(middle_ref[rows, :], turn, 1)
        side = pltpu.roll(side_ref[rows, :], turn, 1)
        within = (lane + dx >= 0) & (lane + dx < LANES)
        inner_s = jnp.where(within, middle, side)
        edge_s = jnp.where(within, side, middle).astype(BF16)
        mean_s, gain_s = statistics(inner_s[EDGE : EDGE + PATCH_SIDE])
        inner_s = inner_s.astype(BF16)

        around, around_inner = spectra(inner_a, edge_a, mean_a, table, "around", 2)
        search, search_inner = spectra(inner_s, edge_s, mean_s, table, "search", 1)
        scale = valid[k].astype(F32) / (2.0 * PATCH_SIDE * CYCLE * CYCLE)
        gain_a, gain_s = gain_a * scale, gain_s * scale
        a, b, c, d = [
            gain_a * ahead + gain_s * behind
            for ahead, behind in zip(matched(search, around_inner), matched(search_inner, around))
        ]
        spectrum = jnp.concatenate(
            [jnp.concatenate([a, c], axis=1), jnp.concatenate([b, d], axis=1)], axis=0
        )
        lines = dot(table["back_down"][...], thrice(spectrum))
        high, low = two(lines)
        surface = dot(jnp.concatenate([high, low, high], axis=1), table["back_across"][...])
        half = SHIFTS // 2
        out_ref[k] = jnp.where(halves, surface[:half], surface[half:])
        return carry

    lax.fori_loop(0, patch_count, one, 0)


def surfaces(first, gathered, owner, tile, offset, valid):
    patch_count = owner.shape[0]
    made = tables()
    return pl.pallas_call(
        kernel,
        out_shape=jax.ShapeDtypeStruct((patch_count, SHIFTS // 2, 2 * SHIFTS), F32),
        in_specs=[pl.BlockSpec(memory_space=pltpu.SMEM)] * 4
        + [pl.BlockSpec(memory_space=pltpu.VMEM)] * (2 + len(NAMES)),
        out_specs=pl.BlockSpec(memory_space=pltpu.VMEM),
        scratch_shapes=[pltpu.VMEM((ROWS, LANES), F32)] * 2,
    )(owner, tile, offset, valid, first, gathered, *[jnp.asarray(made[n]) for n in NAMES])


def exchange(bands, strips, first, second, wide, gathered, zeros, *sems):
    near_send, near_recv, side_send, side_recv, plane_send, plane_recv = sems[:6]
    band_send, band_recv, pair_send, pair_recv, edge_send, edge_recv, local = sems[6:]
    band, strip = lax.axis_index("band"), lax.axis_index("strip")
    rows, cols = second.shape
    core = strip % 2

    def flip(value, bit):
        return value + bit * (1 - 2 * (value // bit % 2))

    pair = flip(strip, 1)
    bits = [1 << i for i in range(1, strips.bit_length() - 1)]
    turned = bits[1:] + bits[:1]

    def step(value, i):
        return flip(value, bits[i]) * (1 - core) + flip(value, turned[i]) * core

    def remote(source, target, send, recv, to):
        return pltpu.make_async_remote_copy(
            src_ref=source,
            dst_ref=target,
            send_sem=send,
            recv_sem=recv,
            device_id=to,
            device_id_type=pl.DeviceIdType.MESH,
        )

    has_up, has_down = band > 0, band < bands - 1
    has_left, has_right = strip > 0, strip < strips - 1
    up, down = (band - 1, strip), (band + 1, strip)
    left, right = (band, strip - 1), (band, strip + 1)
    peers = [(None, (band, pair))] + [(None, (band, step(strip, i))) for i in range(len(bits))]
    peers += [(has_up, up), (has_down, down), (has_left, left), (has_right, right)]

    barrier = pltpu.get_barrier_semaphore()
    for there, peer in peers:
        if there is None:
            pl.semaphore_signal(barrier, inc=1, device_id=peer, device_id_type=pl.DeviceIdType.MESH)
        else:

            @pl.when(there)
            def _():
                pl.semaphore_signal(
                    barrier, inc=1, device_id=peer, device_id_type=pl.DeviceIdType.MESH
                )

    zeros[...] = jnp.zeros_like(zeros)
    present = [1 if there is None else there.astype(jnp.int32) for there, _ in peers]
    pl.semaphore_wait(barrier, sum(present))

    inner_rows, inner_cols = pl.ds(EDGE, rows), pl.ds(LANES, cols)
    top_rows, bottom_rows = pl.ds(0, EDGE), pl.ds(EDGE + rows, EDGE)
    own_first = pltpu.make_async_copy(first, wide.at[inner_rows, inner_cols], local.at[0])
    own_second = pltpu.make_async_copy(second, gathered.at[strip, pl.ds(HALO, rows), :], local.at[1])
    near_up = remote(
        first.at[pl.ds(0, EDGE), :],
        wide.at[bottom_rows, inner_cols],
        near_send.at[0],
        near_recv.at[0],
        up,
    )
    near_down = remote(
        first.at[pl.ds(rows - EDGE, EDGE), :],
        wide.at[top_rows, inner_cols],
        near_send.at[1],
        near_recv.at[1],
        down,
    )
    own_first.start()

    def when(there, action):
        if there is None:
            action()
        else:
            pl.when(there)(action)

    when(has_up, near_up.start)
    when(has_down, near_down.start)

    middle = (rows - 2 * HALO) // 3
    spans = [(0, HALO), (rows - HALO, HALO)]
    spans += [(HALO + i * middle, middle) for i in range(3)]
    held = [strip]

    def piece(block, q):
        low, size = spans[q]
        return gathered.at[block, pl.ds(HALO + low, size), :]

    def halo(block, side):
        return gathered.at[block, pl.ds(HALO + rows if side == 0 else 0, HALO), :]

    pending = []

    def along_band(j, q, source):
        low, size = spans[q]
        to, there = (up, has_up) if q == 0 else (down, has_down)
        copy = remote(source, halo(held[j], q), band_send.at[j, q], band_recv.at[j, q], to)
        when(there, copy.start)
        pending.append((there, copy.wait_send))

    def to_pair(j, q, source):
        copy = remote(
            source, piece(held[j], q), pair_send.at[j, q], pair_recv.at[j, q], (band, pair)
        )
        copy.start()
        pending.append((None, copy.wait_send))
        pending.append((None, copy.wait_recv))

    arriving = {}

    def in_plane(j, q, i, source):
        new = j + (1 << i)
        copy = remote(
            source,
            piece(held[j], q),
            plane_send.at[new, q],
            plane_recv.at[new, q],
            (band, step(strip, i)),
        )
        copy.start()
        pending.append((None, copy.wait_send))
        arriving[new, q] = copy

    for q, (low, size) in enumerate(spans):
        source = second.at[pl.ds(low, size), :]
        for i in range(len(bits)):
            in_plane(0, q, i, source)
        if q < 2:
            along_band(0, q, source)
        to_pair(0, q, source)
    own_second.start()

    top_zero = pltpu.make_async_copy(zeros.at[pl.ds(0, EDGE), :], wide.at[top_rows, inner_cols], local.at[2])
    bottom_zero = pltpu.make_async_copy(
        zeros.at[pl.ds(0, EDGE), :], wide.at[bottom_rows, inner_cols], local.at[3]
    )
    absent = [(band == 0, top_zero), (band == bands - 1, bottom_zero)]
    left_zero = pltpu.make_async_copy(
        zeros.at[:, pl.ds(0, LANES)], wide.at[:, pl.ds(0, LANES)], local.at[4]
    )
    right_zero = pltpu.make_async_copy(
        zeros.at[:, pl.ds(0, LANES)], wide.at[:, pl.ds(LANES + cols, LANES)], local.at[5]
    )
    late = [(strip == 0, left_zero), (strip == strips - 1, right_zero)]
    for block in range(strips):
        for side in range(2):
            fill = pltpu.make_async_copy(
                zeros.at[pl.ds(0, HALO), :], halo(block, side), local.at[6 + 2 * block + side]
            )
            late.append((band == (bands - 1 if side == 0 else 0), fill))
    for there, fill in absent + late:
        when(there, fill.start)

    own_first.wait()
    for there, fill in absent:
        when(there, fill.wait)
    when(has_down, near_up.wait_recv)
    when(has_up, near_down.wait_recv)
    side_right = remote(
        wide.at[:, pl.ds(cols, LANES)],
        wide.at[:, pl.ds(0, LANES)],
        side_send.at[0],
        side_recv.at[0],
        right,
    )
    side_left = remote(
        wide.at[:, pl.ds(LANES, LANES)],
        wide.at[:, pl.ds(LANES + cols, LANES)],
        side_send.at[1],
        side_recv.at[1],
        left,
    )
    when(has_right, side_right.start)
    when(has_left, side_left.start)

    for i in range(len(bits)):
        held += [step(value, i) for value in held]

    order = []
    for i in range(len(bits)):
        group = [j for j in range(1, len(held)) if bin(j).count("1") == i + 1]
        order += [(j, q) for q in range(len(spans)) for j in group]
    for j, q in order:
        arriving[j, q].wait_recv()
        source = piece(held[j], q)
        for i in range(j.bit_length(), len(bits)):
            in_plane(j, q, i, source)
        if q < 2:
            along_band(j, q, source)
        to_pair(j, q, source)

    for j in range(len(held)):
        for side, there in ((0, has_down), (1, has_up)):
            target = halo(held[j], side)
            seen = remote(
                target, target, band_send.at[j, side], band_recv.at[j, side], (band, pair)
            )
            copy = remote(
                target, target, edge_send.at[j, side], edge_recv.at[j, side], (band, pair)
            )
            when(there, seen.wait_recv)
            when(there, copy.start)
            pending.append((there, copy.wait_send))
            pending.append((there, copy.wait_recv))

    when(has_left, side_right.wait_recv)
    when(has_right, side_left.wait_recv)
    when(has_right, side_right.wait_send)
    when(has_left, side_left.wait_send)
    when(has_up, near_up.wait_send)
    when(has_down, near_down.wait_send)
    own_second.wait()
    for there, fill in late:
        when(there, fill.wait)
    for there, wait in pending:
        when(there, wait)


def gather(bands, strips, first, second):
    rows, cols = second.shape
    held = max(strips // 2, 1)
    dma = pltpu.SemaphoreType.DMA
    return pl.pallas_call(
        functools.partial(exchange, bands, strips),
        out_shape=(
            jax.ShapeDtypeStruct((rows + 2 * EDGE, cols + 2 * LANES), first.dtype),
            jax.ShapeDtypeStruct((strips, rows + 2 * HALO, cols), second.dtype),
        ),
        in_specs=[pl.BlockSpec(memory_space=pltpu.VMEM)] * 2,
        out_specs=[pl.BlockSpec(memory_space=pl.ANY)] * 2,
        scratch_shapes=[
            pltpu.VMEM((rows + 2 * EDGE, cols), second.dtype),
            dma((2,)),
            dma((2,)),
            dma((2,)),
            dma((2,)),
            dma((held, 5)),
            dma((held, 5)),
            dma((held, 2)),
            dma((held, 2)),
            dma((held, 5)),
            dma((held, 5)),
            dma((held, 2)),
            dma((held, 2)),
            dma((6 + 2 * strips,)),
        ],
        compiler_params=pltpu.CompilerParams(collective_id=0, has_side_effects=True),
    )(first, second)


def on_device(bands, strips, first_scene, second_scene, owner_strip, target_tile, offsets, valid_mask):
    patch_count = target_tile.shape[-1]
    wide, gathered = gather(bands, strips, first_scene, second_scene)
    result = surfaces(
        wide,
        gathered,
        owner_strip.reshape(patch_count),
        target_tile.reshape(patch_count),
        offsets.reshape(2 * patch_count),
        valid_mask.reshape(patch_count),
    )
    return result.reshape(1, 1, patch_count, SHIFTS * SHIFTS)


def solution(mesh):
    return jax.shard_map(
        functools.partial(on_device, mesh.shape["band"], mesh.shape["strip"]),
        mesh=mesh,
        in_specs=(
            P("band", "strip"),
            P("band", "strip"),
            P("band", "strip", None, None),
            P("band", "strip", None),
            P("band", "strip", None, None),
            P("band", "strip", None),
        ),
        out_specs=P("band", "strip", None, None),
        check_vma=False,
    )
```

```python
import functools

import jax
import jax.numpy as jnp
import numpy as np
from jax import lax
from jax.experimental import pallas as pl
from jax.experimental.pallas import tpu as pltpu
from jax.sharding import PartitionSpec as P

PATCH_SIDE = 128
SHIFTS = 64
EDGE = SHIFTS // 2
SEARCH = PATCH_SIDE + SHIFTS
CYCLE = SEARCH - 1
BINS = (CYCLE + 1) // 2
LANES = 128
WIDE = 2 * LANES
HALO = 64
ROWS = SEARCH + 16
SPLIT = 3
GROUPS = 4
EACH = 2
EPSILON = 1e-05
F32 = jnp.float32
BF16 = jnp.bfloat16


def two(x):
    high = x.astype(BF16)
    return high, (x - high.astype(F32)).astype(BF16)


def two_np(x):
    high = x.astype(jnp.bfloat16)
    low = (x - high.astype(np.float64)).astype(jnp.bfloat16)
    return high, low


def tables():
    angle = 2 * np.pi / CYCLE
    freq = np.arange(BINS)

    def across(place, real):
        out = np.zeros((LANES, WIDE))
        phase = angle * place[:, None] * freq[None, :]
        out[:, :BINS] = np.cos(phase) * real[:, None]
        out[:, LANES : LANES + BINS] = np.sin(phase) * real[:, None]
        return out

    def down(place, real):
        phase = angle * place[None, :] * freq[:, None]
        return np.concatenate([np.cos(phase), np.sin(phase)], axis=0) * real[None, :]

    lane = np.arange(LANES)
    edge_place = np.where(lane < LANES // 2, PATCH_SIDE + lane, lane - LANES)
    row = np.arange(SEARCH) - EDGE
    made = {}
    sums = []
    inner = across(lane, np.ones(LANES))
    high, low = two_np(inner)
    made["inner"] = np.concatenate([high, low], axis=0)
    sums.append((high.astype(np.float64) + low.astype(np.float64)).sum(0))
    high, low = two_np(down(row[EDGE : EDGE + PATCH_SIDE], np.ones(PATCH_SIDE)))
    made["down_inner"] = np.concatenate([high, high, low], axis=1)
    for name, first, last in (("search", -EDGE, CYCLE - EDGE), ("around", 1 - EDGE, CYCLE - EDGE + 1)):
        real = (edge_place >= first) & (edge_place < last)
        real &= (lane < EDGE) | (lane >= LANES - EDGE)
        high, low = two_np(across(edge_place, real))
        made["edge_" + name] = np.concatenate([high, low], axis=0)
        sums.append(sums[0] + (high.astype(np.float64) + low.astype(np.float64)).sum(0))
        high, low = two_np(down(row, (row >= first) & (row < last)))
        made["down_" + name] = np.concatenate([high, high, low], axis=1)
    made["sums"] = np.concatenate([np.stack(sums), np.zeros((5, WIDE))], axis=0).astype(np.float32)
    lag = np.concatenate([np.arange(0, SHIFTS, 2), np.arange(1, SHIFTS, 2)]) - EDGE
    weight = np.where(freq == 0, 1.0, 2.0)
    phase = angle * lag[:, None] * freq[None, :]
    back = np.concatenate([np.cos(phase) * weight, np.sin(phase) * weight], axis=1)
    high, low = two_np(back)
    made["back_down"] = np.concatenate([high, high, low], axis=1)
    lag = np.arange(LANES) % SHIFTS - EDGE
    phase = angle * freq[:, None] * lag[None, :]
    back = np.zeros((WIDE, LANES))
    back[:BINS] = np.cos(phase) * weight[:, None]
    back[LANES : LANES + BINS] = np.sin(phase) * weight[:, None]
    high, low = two_np(back)
    made["back_across"] = np.concatenate([high, high, low], axis=0)
    return made


FORMER = ("inner", "edge_around", "down_inner", "down_around", "sums")
LATTER = (
    "inner",
    "edge_search",
    "down_inner",
    "down_search",
    "back_down",
    "back_across",
    "sums",
)


def dot(a, b):
    return jnp.dot(a, b, preferred_element_type=F32)


def thrice(x):
    high, low = two(x)
    return jnp.concatenate([high, low, high], axis=0)


def statistics(patch):
    count = PATCH_SIDE * PATCH_SIDE
    mean = jnp.sum(patch) / count
    centered = patch - mean
    return mean, lax.rsqrt(jnp.full((1, LANES), jnp.sum(centered * centered) / count + EPSILON))


def spectra(inner, edge, mean, table, name, row):
    core = dot(jnp.concatenate([inner, inner], axis=1), table["inner"][...])
    rim = dot(jnp.concatenate([edge, edge], axis=1), table["edge_" + name][...])
    sums = table["sums"]
    full = core + rim - mean * sums[row : row + 1, :]
    core = core[EDGE : EDGE + PATCH_SIDE] - mean * sums[0:1, :]
    return dot(table["down_" + name][...], thrice(full)), dot(table["down_inner"][...], thrice(core))


def quarters(x):
    return x[:BINS, :LANES], x[BINS:, :LANES], x[:BINS, LANES:], x[BINS:, LANES:]


def matched(x, y):
    x0, x1, x2, x3 = quarters(x)
    y0, y1, y2, y3 = quarters(y)
    return (
        x0 * y0 + x1 * y1 + x2 * y2 + x3 * y3,
        x1 * y0 - x0 * y1 + x3 * y2 - x2 * y3,
        x2 * y0 - x0 * y2 + x3 * y1 - x1 * y3,
        x0 * y3 + x3 * y0 - x1 * y2 - x2 * y1,
    )


def flip(value, bit):
    return value + bit * (1 - 2 * (value // bit % 2))


def remote(source, target, send, recv, to):
    return pltpu.make_async_remote_copy(
        src_ref=source,
        dst_ref=target,
        send_sem=send,
        recv_sem=recv,
        device_id=to,
        device_id_type=pl.DeviceIdType.MESH,
    )


def when(there, action):
    if there is None:
        action()
    else:
        pl.when(there)(action)


def exchange(bands, strips, first, second, *refs):
    refs = list(refs)

    def take(count):
        taken, refs[:count] = refs[:count], []
        return taken

    stored = take(len(FORMER))
    gathered, around_out, core_out = take(3)
    wide, around_ref, core_ref, zeros = take(4)
    table_refs = take(len(FORMER))
    near_send, near_recv, plane_send, plane_recv, band_send, band_recv = take(6)
    pair_send, pair_recv, edge_send, edge_recv, local, table_sem, out_sem, fill_sem = take(8)
    table = dict(zip(FORMER, table_refs))

    band, strip = lax.axis_index("band"), lax.axis_index("strip")
    rows, cols = second.shape
    patch_count = around_ref.shape[0]
    per_row = cols // LANES
    core = strip % 2
    pair = flip(strip, 1)
    bits = [1 << i for i in range(1, strips.bit_length() - 1)]
    turned = bits[1:] + bits[:1]

    def step(value, i):
        return flip(value, bits[i]) * (1 - core) + flip(value, turned[i]) * core

    has_up, has_down = band > 0, band < bands - 1
    has_left, has_right = strip > 0, strip < strips - 1
    near = []
    for dr in (-1, 0, 1):
        for dc in (-1, 0, 1):
            if dr == 0 and dc == 0:
                continue
            there = None
            for wanted in ([has_up] if dr < 0 else [has_down] if dr > 0 else []) + (
                [has_left] if dc < 0 else [has_right] if dc > 0 else []
            ):
                there = wanted if there is None else there & wanted
            near.append((dr, dc, there))
    peers = [(None, (band, pair))] + [(None, (band, step(strip, i))) for i in range(len(bits))]
    peers += [(there, (band + dr, strip + dc)) for dr, dc, there in near]

    barrier = pltpu.get_barrier_semaphore()
    for there, peer in peers:

        def signal(peer=peer):
            pl.semaphore_signal(barrier, inc=1, device_id=peer, device_id_type=pl.DeviceIdType.MESH)

        when(there, signal)

    locals_ = [
        pltpu.make_async_copy(
            first, wide.at[pl.ds(EDGE, rows), pl.ds(LANES, cols)], local.at[0]
        ),
        pltpu.make_async_copy(second, gathered.at[strip, pl.ds(HALO, rows), :], local.at[1]),
    ]
    locals_ += [
        pltpu.make_async_copy(source, target, table_sem.at[i])
        for i, (source, target) in enumerate(zip(stored, table_refs))
    ]
    for copy in locals_:
        copy.start()

    def row_blank(low):
        wide[pl.ds(low, EDGE), :] = jnp.zeros((EDGE, cols + 2 * LANES), wide.dtype)

    def col_blank(low):
        wide[pl.ds(EDGE, rows), pl.ds(low, LANES)] = jnp.zeros((rows, LANES), wide.dtype)

    def corner_blank(there, low, left):
        @pl.when(there)
        def _():
            wide[pl.ds(low, EDGE), pl.ds(left, LANES)] = jnp.zeros((EDGE, LANES), wide.dtype)

    def halo(block, side):
        return gathered.at[block, pl.ds(HALO + rows if side == 0 else 0, HALO), :]

    zeros[...] = jnp.zeros_like(zeros)
    when(band == 0, lambda: row_blank(0))
    when(band == bands - 1, lambda: row_blank(EDGE + rows))
    when(strip == 0, lambda: col_blank(0))
    when(strip == strips - 1, lambda: col_blank(LANES + cols))
    corner_blank((strip == 0) & has_up, 0, 0)
    corner_blank((strip == 0) & has_down, EDGE + rows, 0)
    corner_blank((strip == strips - 1) & has_up, 0, LANES + cols)
    corner_blank((strip == strips - 1) & has_down, EDGE + rows, LANES + cols)

    present = [1 if there is None else there.astype(jnp.int32) for there, _ in peers]
    pl.semaphore_wait(barrier, sum(present))

    pending = []

    def part(delta, low, full, margin):
        if delta < 0:
            return pl.ds(low, margin)
        if delta > 0:
            return pl.ds(low + full - margin, margin)
        return pl.ds(low, full)

    def beyond(delta, full, margin):
        if delta < 0:
            return pl.ds(margin + full, margin)
        if delta > 0:
            return pl.ds(0, margin)
        return pl.ds(margin, full)

    nearby = []
    for i, (dr, dc, there) in enumerate(near):
        copy = remote(
            first.at[part(dr, 0, rows, EDGE), part(dc, 0, cols, LANES)],
            wide.at[beyond(dr, rows, EDGE), beyond(dc, cols, LANES)],
            near_send.at[i],
            near_recv.at[i],
            (band + dr, strip + dc),
        )
        when(there, copy.start)
        pending.append((there, copy.wait_send))
        back = [t for r, c, t in near if r == -dr and c == -dc][0]
        nearby.append((back, copy.wait_recv))

    middle = (rows - 2 * HALO) // SPLIT
    spans = [(0, HALO), (rows - HALO, HALO)]
    spans += [(HALO + i * middle, middle) for i in range(SPLIT)]
    held = [strip]

    def piece(block, q):
        low, size = spans[q]
        return gathered.at[block, pl.ds(HALO + low, size), :]

    def along_band(j, q, source):
        to, there = (up, has_up) if q == 0 else (down, has_down)
        copy = remote(source, halo(held[j], q), band_send.at[j, q], band_recv.at[j, q], to)
        when(there, copy.start)
        pending.append((there, copy.wait_send))

    up, down = (band - 1, strip), (band + 1, strip)
    to_mate = (band, pair)

    def to_pair(j, q, source):
        copy = remote(source, piece(held[j], q), pair_send.at[j, q], pair_recv.at[j, q], to_mate)
        copy.start()
        pending.append((None, copy.wait_send))
        pending.append((None, copy.wait_recv))

    arriving = {}

    def in_plane(j, q, i, source):
        new = j + (1 << i)
        copy = remote(
            source,
            piece(held[j], q),
            plane_send.at[new, q],
            plane_recv.at[new, q],
            (band, step(strip, i)),
        )
        copy.start()
        pending.append((None, copy.wait_send))
        arriving[new, q] = copy

    for q, (low, size) in enumerate(spans):
        source = second.at[pl.ds(low, size), :]
        for i in range(len(bits)):
            in_plane(0, q, i, source)
        if q < 2:
            along_band(0, q, source)
        to_pair(0, q, source)

    for i in range(len(bits)):
        held += [step(value, i) for value in held]

    order = []
    for i in range(len(bits)):
        group = [j for j in range(1, len(held)) if bin(j).count("1") == i + 1]
        order += [(j, q) for q in range(len(spans)) for j in group]

    def forward(j, q):
        arriving[j, q].wait_recv()
        source = piece(held[j], q)
        for i in range(j.bit_length(), len(bits)):
            in_plane(j, q, i, source)
        if q < 2:
            along_band(j, q, source)
        to_pair(j, q, source)

    for block in range(strips):
        for side in range(2):
            fill = pltpu.make_async_copy(zeros, halo(block, side), fill_sem.at[block, side])
            absent = band == (bands - 1 if side == 0 else 0)
            when(absent, fill.start)
            pending.append((absent, fill.wait))
    for there, wait in nearby:
        when(there, wait)
    locals_[0].wait()
    for copy in locals_[2:]:
        copy.wait()
    pending.append((None, locals_[1].wait))

    lane = lax.broadcasted_iota(jnp.int32, (1, LANES), 1)
    halves = lane < LANES // 2

    def place_of(c):
        return pl.ds(pl.multiple_of(c * LANES, LANES), LANES)

    def results(k):
        return [
            pltpu.make_async_copy(source.at[k], target.at[k], out_sem.at[i, k])
            for i, (source, target) in enumerate(((around_ref, around_out), (core_ref, core_out)))
        ]

    def around_one(k, carry):
        top = pl.multiple_of(k // per_row * PATCH_SIDE, 16)
        window = pl.ds(top, SEARCH)
        here = k % per_row
        inner = wide[window, place_of(here + 1)]
        edge = jnp.where(halves, wide[window, place_of(here + 2)], wide[window, place_of(here)])
        mean, gain = statistics(inner[EDGE : EDGE + PATCH_SIDE].astype(F32))
        full, inside = spectra(inner, edge, mean, table, "around", 2)
        around_ref[k] = full
        core_ref[k] = inside * gain[:, :1]
        for copy in results(k):
            copy.start()
        return carry

    done = 0
    steps = len(order)
    groups = GROUPS
    for g in range(groups):
        lax.fori_loop(g * patch_count // groups, (g + 1) * patch_count // groups, around_one, 0)
        upto = (g + 1) * steps // groups
        for j, q in order[done:upto]:
            forward(j, q)
        done = upto

    for j in range(len(held)):
        for side, there in ((0, has_down), (1, has_up)):
            target = halo(held[j], side)
            seen = remote(target, target, band_send.at[j, side], band_recv.at[j, side], to_mate)
            copy = remote(target, target, edge_send.at[j, side], edge_recv.at[j, side], to_mate)
            when(there, seen.wait_recv)
            when(there, copy.start)
            pending.append((there, copy.wait_send))
            pending.append((there, copy.wait_recv))
    for there, wait in pending:
        when(there, wait)

    for k in range(patch_count):
        for copy in results(k):
            copy.wait()


def correlate(rows_total, owner, tile, offset, valid, gathered, around_ref, core_ref, *refs):
    table = dict(zip(LATTER, refs[: len(LATTER)]))
    out_ref, blocks, middle_ref, side_ref, surface_ref, sems = refs[len(LATTER) :]
    turn_id = pl.program_id(0)
    patch_count = out_ref.shape[0]
    each = around_ref.shape[0]
    per_row = gathered.shape[2] // LANES
    tiles = gathered.shape[0] * per_row
    lane = lax.broadcasted_iota(jnp.int32, (1, LANES), 1)
    halves = lane < LANES // 2
    half = SHIFTS // 2

    def place_of(k):
        place = owner[k] * per_row + tile[k] % per_row
        row = tile[k] // per_row * PATCH_SIDE + HALO - EDGE + offset[0, k]
        return place, row, jnp.minimum(row // 16 * 16, rows_total - ROWS)

    def fetch(turn, slot):
        made = []
        for n in range(each):
            place, _, base = place_of(turn * each + n)
            for c in range(3):
                block = jnp.minimum(jnp.maximum(place + c - 1, 0), tiles - 1)
                made.append(
                    pltpu.make_async_copy(
                        gathered.at[
                            block // per_row,
                            pl.ds(pl.multiple_of(base, 16), ROWS),
                            pl.ds(pl.multiple_of(block % per_row * LANES, LANES), LANES),
                        ],
                        blocks.at[slot, n, c],
                        sems.at[slot, n, c],
                    )
                )
        return made

    slot = turn_id % 2

    @pl.when(turn_id == 0)
    def _():
        for copy in fetch(0, 0):
            copy.start()

    @pl.when(turn_id + 1 < pl.num_programs(0))
    def _():
        for copy in fetch(turn_id + 1, 1 - slot):
            copy.start()

    for copy in fetch(turn_id, slot):
        copy.wait()

    for n in range(each):
        k = turn_id * each + n
        place, row, base = place_of(k)
        right_end = jnp.where(place == tiles - 1, 0, LANES // 2)
        left_start = jnp.where(place == 0, LANES, LANES // 2)
        middle_ref[n] = blocks[slot, n, 1].astype(F32)
        side_ref[n] = jnp.where(
            lane < right_end,
            blocks[slot, n, 2].astype(F32),
            jnp.where(lane >= left_start, blocks[slot, n, 0].astype(F32), 0.0),
        )
        shown = pl.ds(row - base, SEARCH)
        dx = offset[1, k]
        turn = jnp.where(dx > 0, LANES - dx, -dx)
        centre = pltpu.roll(middle_ref[n, shown, :], turn, 1)
        side = pltpu.roll(side_ref[n, shown, :], turn, 1)
        within = (lane + dx >= 0) & (lane + dx < LANES)
        inner = jnp.where(within, centre, side)
        edge = jnp.where(within, side, centre).astype(BF16)
        mean, gain = statistics(inner[EDGE : EDGE + PATCH_SIDE])
        full, inside = spectra(inner.astype(BF16), edge, mean, table, "search", 1)
        inside = inside * gain[:, :1]
        a, b, c, d = [
            ahead + behind
            for ahead, behind in zip(matched(full, core_ref[n]), matched(inside, around_ref[n]))
        ]
        spectrum = jnp.concatenate(
            [jnp.concatenate([a, c], axis=1), jnp.concatenate([b, d], axis=1)], axis=0
        )
        lines = dot(table["back_down"][...], thrice(spectrum))
        high, low = two(lines)
        surface = dot(jnp.concatenate([high, low, high], axis=1), table["back_across"][...])
        scale = valid[k].astype(F32) / (2.0 * PATCH_SIDE * CYCLE * CYCLE)
        surface_ref[pl.ds(pl.multiple_of(k * half, half), half), :] = (
            jnp.where(halves, surface[:half], surface[half:]) * scale
        )

    @pl.when(turn_id == pl.num_programs(0) - 1)
    def _():
        for r in range(half):
            out_ref[:, r * LANES : (r + 1) * LANES] = surface_ref[
                pl.ds(r, patch_count, stride=half), :
            ]


def on_device(bands, strips, first_scene, second_scene, owner_strip, target_tile, offsets, valid_mask):
    patch_count = target_tile.shape[-1]
    rows, cols = second_scene.shape
    made = tables()
    former = [jnp.asarray(made[name]) for name in FORMER]
    latter = [jnp.asarray(made[name]) for name in LATTER]
    held = max(strips // 2, 1)
    dma = pltpu.SemaphoreType.DMA
    pieces = SPLIT + 2
    spectrum = (patch_count, 2 * BINS, WIDE)
    gathered, around, core = pl.pallas_call(
        functools.partial(exchange, bands, strips),
        out_shape=(
            jax.ShapeDtypeStruct((strips, rows + 2 * HALO, cols), second_scene.dtype),
            jax.ShapeDtypeStruct(spectrum, F32),
            jax.ShapeDtypeStruct(spectrum, F32),
        ),
        in_specs=[pl.BlockSpec(memory_space=pl.ANY)] * (2 + len(FORMER)),
        out_specs=[pl.BlockSpec(memory_space=pl.ANY)] * 3,
        scratch_shapes=[
            pltpu.VMEM((rows + 2 * EDGE, cols + 2 * LANES), first_scene.dtype),
            pltpu.VMEM(spectrum, F32),
            pltpu.VMEM(spectrum, F32),
            pltpu.VMEM((HALO, cols), second_scene.dtype),
            *[pltpu.VMEM(c.shape, c.dtype) for c in former],
            dma((8,)),
            dma((8,)),
            dma((held, pieces)),
            dma((held, pieces)),
            dma((held, 2)),
            dma((held, 2)),
            dma((held, pieces)),
            dma((held, pieces)),
            dma((held, 2)),
            dma((held, 2)),
            dma((2,)),
            dma((len(FORMER),)),
            dma((2, patch_count)),
            dma((strips, 2)),
        ],
        compiler_params=pltpu.CompilerParams(collective_id=0, has_side_effects=True),
    )(first_scene, second_scene, *former)
    each = EACH
    block = pl.BlockSpec((each,) + spectrum[1:], lambda k, *_: (k, 0, 0))
    result = pl.pallas_call(
        functools.partial(correlate, rows + 2 * HALO),
        out_shape=jax.ShapeDtypeStruct((patch_count, SHIFTS * SHIFTS), F32),
        grid_spec=pltpu.PrefetchScalarGridSpec(
            num_scalar_prefetch=4,
            grid=(patch_count // each,),
            in_specs=[pl.BlockSpec(memory_space=pl.ANY), block, block]
            + [pl.BlockSpec(c.shape, lambda k, *_: (0, 0)) for c in latter],
            out_specs=pl.BlockSpec((patch_count, SHIFTS * SHIFTS), lambda k, *_: (0, 0)),
            scratch_shapes=[
                pltpu.VMEM((2, each, 3, ROWS, LANES), second_scene.dtype),
                pltpu.VMEM((each, ROWS, LANES), F32),
                pltpu.VMEM((each, ROWS, LANES), F32),
                pltpu.VMEM((patch_count * SHIFTS // 2, LANES), F32),
                dma((2, each, 3)),
            ],
        ),
    )(
        owner_strip.reshape(patch_count),
        target_tile.reshape(patch_count),
        offsets.reshape(patch_count, 2).T,
        valid_mask.reshape(patch_count),
        gathered,
        around,
        core,
        *latter,
    )
    return result.reshape(1, 1, patch_count, SHIFTS * SHIFTS)


def solution(mesh):
    return jax.shard_map(
        functools.partial(on_device, mesh.shape["band"], mesh.shape["strip"]),
        mesh=mesh,
        in_specs=(
            P("band", "strip"),
            P("band", "strip"),
            P("band", "strip", None, None),
            P("band", "strip", None),
            P("band", "strip", None, None),
            P("band", "strip", None),
        ),
        out_specs=P("band", "strip", None, None),
        check_vma=False,
    )
```

```python
import functools

import jax
import jax.numpy as jnp
import numpy as np
from jax import lax
from jax.experimental import pallas as pl
from jax.experimental.pallas import tpu as pltpu
from jax.sharding import PartitionSpec as P

PATCH_SIDE = 128
SHIFTS = 64
EDGE = SHIFTS // 2
SEARCH = PATCH_SIDE + SHIFTS
CYCLE = SEARCH - 1
BINS = (CYCLE + 1) // 2
LANES = 128
WIDE = 2 * LANES
HALO = 64
ROWS = SEARCH + 16
SPLIT = 3
EACH = 4
EPSILON = 1e-05
F32 = jnp.float32
BF16 = jnp.bfloat16


def two(x):
    high = x.astype(BF16)
    return high, (x - high.astype(F32)).astype(BF16)


def two_np(x):
    high = x.astype(jnp.bfloat16)
    low = (x - high.astype(np.float64)).astype(jnp.bfloat16)
    return high, low


def tables():
    angle = 2 * np.pi / CYCLE
    freq = np.arange(BINS)

    def across(place, real):
        out = np.zeros((LANES, WIDE))
        phase = angle * place[:, None] * freq[None, :]
        out[:, :BINS] = np.cos(phase) * real[:, None]
        out[:, LANES : LANES + BINS] = np.sin(phase) * real[:, None]
        return out

    def down(place, real):
        phase = angle * place[None, :] * freq[:, None]
        return np.concatenate([np.cos(phase), np.sin(phase)], axis=0) * real[None, :]

    lane = np.arange(LANES)
    edge_place = np.where(lane < LANES // 2, PATCH_SIDE + lane, lane - LANES)
    row = np.arange(SEARCH) - EDGE
    made = {}
    sums = []
    inner = across(lane, np.ones(LANES))
    high, low = two_np(inner)
    made["inner"] = np.concatenate([high, low], axis=0)
    sums.append((high.astype(np.float64) + low.astype(np.float64)).sum(0))
    high, low = two_np(down(row[EDGE : EDGE + PATCH_SIDE], np.ones(PATCH_SIDE)))
    made["down_inner"] = np.concatenate(
        [np.concatenate([high, high], axis=1), np.concatenate([low, low], axis=1)], axis=0
    )
    for name, first, last in (("search", -EDGE, CYCLE - EDGE), ("around", 1 - EDGE, CYCLE - EDGE + 1)):
        real = (edge_place >= first) & (edge_place < last)
        real &= (lane < EDGE) | (lane >= LANES - EDGE)
        high, low = two_np(across(edge_place, real))
        made["edge_" + name] = np.concatenate([high, low], axis=0)
        sums.append(sums[0] + (high.astype(np.float64) + low.astype(np.float64)).sum(0))
        high, low = two_np(down(row, (row >= first) & (row < last)))
        made["down_" + name] = np.concatenate([high, low], axis=0)
    made["sums"] = np.concatenate([np.stack(sums), np.zeros((5, WIDE))], axis=0).astype(np.float32)
    lag = np.concatenate([np.arange(0, SHIFTS, 2), np.arange(1, SHIFTS, 2)]) - EDGE
    weight = np.where(freq == 0, 1.0, 2.0)
    phase = angle * lag[:, None] * freq[None, :]
    back = np.concatenate([np.cos(phase) * weight, np.sin(phase) * weight], axis=1)
    high, low = two_np(back)
    made["back_down"] = np.concatenate([high, low], axis=0)
    lag = np.arange(LANES) % SHIFTS - EDGE
    phase = angle * freq[:, None] * lag[None, :]
    back = np.zeros((WIDE, LANES))
    back[:BINS] = np.cos(phase) * weight[:, None]
    back[LANES : LANES + BINS] = np.sin(phase) * weight[:, None]
    high, low = two_np(back)
    made["back_across"] = np.concatenate([high, high, low], axis=0)
    return made


FORMER = ("inner", "edge_around", "down_inner", "down_around", "sums")
LATTER = (
    "inner",
    "edge_search",
    "down_inner",
    "down_search",
    "back_down",
    "back_across",
    "sums",
)


def dot(a, b):
    return jnp.dot(a, b, preferred_element_type=F32)


def stacked(table, x):
    high, low = two(x)
    count = table.shape[0] // 2
    both = dot(table[...], high)
    return both[:count] + both[count:] + dot(table[:count, :], low)


def stacked_inner(table, x):
    both = dot(table[...], jnp.concatenate(two(x), axis=0))
    count = both.shape[0] // 2
    return both[:count] + both[count:]


def statistics(patch):
    count = PATCH_SIDE * PATCH_SIDE
    mean = jnp.sum(patch) / count
    centered = patch - mean
    return mean, lax.rsqrt(jnp.full((1, LANES), jnp.sum(centered * centered) / count + EPSILON))


def across(inners, edges, table, name):
    def twice(parts):
        rows = jnp.concatenate(parts, axis=0)
        return jnp.concatenate([rows, rows], axis=1)

    core = dot(twice(inners), table["inner"][...])
    rim = dot(twice(edges), table["edge_" + name][...])
    return [
        (core[n * SEARCH : (n + 1) * SEARCH], rim[n * SEARCH : (n + 1) * SEARCH])
        for n in range(len(inners))
    ]


def spectra(core, rim, mean, table, name, row):
    sums = table["sums"]
    full = core + rim - mean * sums[row : row + 1, :]
    core = core[EDGE : EDGE + PATCH_SIDE] - mean * sums[0:1, :]
    return stacked(table["down_" + name], full), stacked_inner(table["down_inner"], core)


def quarters(x):
    return x[:BINS, :LANES], x[BINS:, :LANES], x[:BINS, LANES:], x[BINS:, LANES:]


def matched(x, y):
    x0, x1, x2, x3 = quarters(x)
    y0, y1, y2, y3 = quarters(y)
    return (
        x0 * y0 + x1 * y1 + x2 * y2 + x3 * y3,
        x1 * y0 - x0 * y1 + x3 * y2 - x2 * y3,
        x2 * y0 - x0 * y2 + x3 * y1 - x1 * y3,
        x0 * y3 + x3 * y0 - x1 * y2 - x2 * y1,
    )


def flip(value, bit):
    return value + bit * (1 - 2 * (value // bit % 2))


def remote(source, target, send, recv, to):
    return pltpu.make_async_remote_copy(
        src_ref=source,
        dst_ref=target,
        send_sem=send,
        recv_sem=recv,
        device_id=to,
        device_id_type=pl.DeviceIdType.MESH,
    )


def when(there, action):
    if there is None:
        action()
    else:
        pl.when(there)(action)


def exchange(bands, strips, first, second, *refs):
    refs = list(refs)

    def take(count):
        taken, refs[:count] = refs[:count], []
        return taken

    stored = take(len(FORMER))
    gathered, around_out, core_out = take(3)
    wide, around_ref, core_ref, zeros = take(4)
    table_refs = take(len(FORMER))
    near_send, near_recv, plane_send, plane_recv, band_send, band_recv = take(6)
    pair_send, pair_recv, edge_send, edge_recv, local, table_sem, out_sem, fill_sem = take(8)
    table = dict(zip(FORMER, table_refs))

    band, strip = lax.axis_index("band"), lax.axis_index("strip")
    rows, cols = second.shape
    patch_count = around_ref.shape[0]
    per_row = cols // LANES
    core = strip % 2
    pair = flip(strip, 1)
    bits = [1 << i for i in range(1, strips.bit_length() - 1)]
    turned = bits[1:] + bits[:1]

    def step(value, i):
        return flip(value, bits[i]) * (1 - core) + flip(value, turned[i]) * core

    has_up, has_down = band > 0, band < bands - 1
    has_left, has_right = strip > 0, strip < strips - 1
    near = []
    for dr in (-1, 0, 1):
        for dc in (-1, 0, 1):
            if dr == 0 and dc == 0:
                continue
            there = None
            for wanted in ([has_up] if dr < 0 else [has_down] if dr > 0 else []) + (
                [has_left] if dc < 0 else [has_right] if dc > 0 else []
            ):
                there = wanted if there is None else there & wanted
            near.append((dr, dc, there))
    peers = [(None, (band, pair))] + [(None, (band, step(strip, i))) for i in range(len(bits))]
    peers += [(there, (band + dr, strip + dc)) for dr, dc, there in near]

    barrier = pltpu.get_barrier_semaphore()
    for there, peer in peers:

        def signal(peer=peer):
            pl.semaphore_signal(barrier, inc=1, device_id=peer, device_id_type=pl.DeviceIdType.MESH)

        when(there, signal)

    locals_ = [
        pltpu.make_async_copy(
            first, wide.at[pl.ds(EDGE, rows), pl.ds(LANES, cols)], local.at[0]
        ),
        pltpu.make_async_copy(second, gathered.at[strip, pl.ds(HALO, rows), :], local.at[1]),
    ]
    locals_ += [
        pltpu.make_async_copy(source, target, table_sem.at[i])
        for i, (source, target) in enumerate(zip(stored, table_refs))
    ]
    for copy in locals_:
        copy.start()

    def row_blank(low):
        wide[pl.ds(low, EDGE), :] = jnp.zeros((EDGE, cols + 2 * LANES), wide.dtype)

    def col_blank(low):
        wide[pl.ds(EDGE, rows), pl.ds(low, LANES)] = jnp.zeros((rows, LANES), wide.dtype)

    def corner_blank(there, low, left):
        @pl.when(there)
        def _():
            wide[pl.ds(low, EDGE), pl.ds(left, LANES)] = jnp.zeros((EDGE, LANES), wide.dtype)

    def halo(block, side):
        return gathered.at[block, pl.ds(HALO + rows if side == 0 else 0, HALO), :]

    zeros[...] = jnp.zeros_like(zeros)
    when(band == 0, lambda: row_blank(0))
    when(band == bands - 1, lambda: row_blank(EDGE + rows))
    when(strip == 0, lambda: col_blank(0))
    when(strip == strips - 1, lambda: col_blank(LANES + cols))
    corner_blank((strip == 0) & has_up, 0, 0)
    corner_blank((strip == 0) & has_down, EDGE + rows, 0)
    corner_blank((strip == strips - 1) & has_up, 0, LANES + cols)
    corner_blank((strip == strips - 1) & has_down, EDGE + rows, LANES + cols)

    present = [1 if there is None else there.astype(jnp.int32) for there, _ in peers]
    pl.semaphore_wait(barrier, sum(present))

    pending = []

    def part(delta, low, full, margin):
        if delta < 0:
            return pl.ds(low, margin)
        if delta > 0:
            return pl.ds(low + full - margin, margin)
        return pl.ds(low, full)

    def beyond(delta, full, margin):
        if delta < 0:
            return pl.ds(margin + full, margin)
        if delta > 0:
            return pl.ds(0, margin)
        return pl.ds(margin, full)

    nearby = []
    for i, (dr, dc, there) in enumerate(near):
        copy = remote(
            first.at[part(dr, 0, rows, EDGE), part(dc, 0, cols, LANES)],
            wide.at[beyond(dr, rows, EDGE), beyond(dc, cols, LANES)],
            near_send.at[i],
            near_recv.at[i],
            (band + dr, strip + dc),
        )
        when(there, copy.start)
        pending.append((there, copy.wait_send))
        back = [t for r, c, t in near if r == -dr and c == -dc][0]
        nearby.append((back, copy.wait_recv))

    middle = (rows - 2 * HALO) // SPLIT
    spans = [(0, HALO), (rows - HALO, HALO)]
    spans += [(HALO + i * middle, middle) for i in range(SPLIT)]
    held = [strip]

    def piece(block, q):
        low, size = spans[q]
        return gathered.at[block, pl.ds(HALO + low, size), :]

    up, down = (band - 1, strip), (band + 1, strip)
    to_mate = (band, pair)

    for i in range(len(bits)):
        held += [step(value, i) for value in held]
    sides = [(band, step(strip, i)) for i in range(len(bits))]
    arriving, onward, leaving = {}, {}, []
    for j in range(len(held)):
        for q, (low, size) in enumerate(spans):
            source = piece(held[j], q) if j else second.at[pl.ds(low, size), :]
            after = []
            for i in range(j.bit_length(), len(bits)):
                new = j + (1 << i)
                copy = remote(
                    source, piece(held[j], q), plane_send.at[new, q], plane_recv.at[new, q], sides[i]
                )
                arriving[new, q] = copy
                after.append((None, copy))
            if q < 2:
                to, there = (up, has_up) if q == 0 else (down, has_down)
                copy = remote(source, halo(held[j], q), band_send.at[j, q], band_recv.at[j, q], to)
                after.append((there, copy))
            copy = remote(source, piece(held[j], q), pair_send.at[j, q], pair_recv.at[j, q], to_mate)
            after.append((None, copy))
            pending.append((None, copy.wait_recv))
            onward[j, q] = after
            pending += [(there, copy.wait_send) for there, copy in after]

    def forward(j, q):
        if j:
            arriving[j, q].wait_recv()
        for there, copy in onward[j, q]:
            when(there, copy.start)

    for q in range(len(spans)):
        forward(0, q)

    for block in range(strips):
        for side in range(2):
            fill = pltpu.make_async_copy(zeros, halo(block, side), fill_sem.at[block, side])
            absent = band == (bands - 1 if side == 0 else 0)
            when(absent, fill.start)
            pending.append((absent, fill.wait))
    for there, wait in nearby:
        when(there, wait)
    locals_[0].wait()
    for copy in locals_[2:]:
        copy.wait()
    pending.append((None, locals_[1].wait))

    lane = lax.broadcasted_iota(jnp.int32, (1, LANES), 1)
    halves = lane < LANES // 2

    def place_of(c):
        return pl.ds(pl.multiple_of(c * LANES, LANES), LANES)

    def results(k):
        return [
            pltpu.make_async_copy(source.at[k], target.at[k], out_sem.at[i, k])
            for i, (source, target) in enumerate(((around_ref, around_out), (core_ref, core_out)))
        ]

    def around_one(k, carry):
        top = pl.multiple_of(k // per_row * PATCH_SIDE, 16)
        window = pl.ds(top, SEARCH)
        here = k % per_row
        inner = wide[window, place_of(here + 1)]
        edge = jnp.where(halves, wide[window, place_of(here + 2)], wide[window, place_of(here)])
        mean, gain = statistics(inner[EDGE : EDGE + PATCH_SIDE].astype(F32))
        ((line, rim),) = across([inner], [edge], table, "around")
        full, inside = spectra(line, rim, mean, table, "around", 2)
        around_ref[k] = full
        core_ref[k] = inside * gain[:, :1]
        for copy in results(k):
            copy.start()
        for at in range(patch_count):
            due = [x for x in order if plan[x] == at]
            if due:

                @pl.when(k == at)
                def _():
                    for j, q in due:
                        forward(j, q)

        return carry

    order = [
        (j, q)
        for n in range(1, len(bits) + 1)
        for q in range(len(spans))
        for j in range(1, len(held))
        if bin(j).count("1") == n
    ]
    plan = {}
    for j, q in order:
        if bin(j).count("1") == 1:
            plan[j, q] = patch_count * (0, 1, 4, 8, 11)[q] // 16
        elif bin(j).count("1") == 2 and q < 2:
            plan[j, q] = patch_count * 14 // 16
        else:
            plan[j, q] = patch_count
    lax.fori_loop(0, patch_count, around_one, 0)
    for j, q in order:
        if plan[j, q] == patch_count:
            forward(j, q)

    for j in range(len(held)):
        for side, there in ((0, has_down), (1, has_up)):
            target = halo(held[j], side)
            seen = remote(target, target, band_send.at[j, side], band_recv.at[j, side], to_mate)
            copy = remote(target, target, edge_send.at[j, side], edge_recv.at[j, side], to_mate)
            when(there, seen.wait_recv)
            when(there, copy.start)
            pending.append((there, copy.wait_send))
            pending.append((there, copy.wait_recv))
    for there, wait in pending:
        when(there, wait)

    for k in range(patch_count):
        for copy in results(k):
            copy.wait()


def correlate(rows_total, owner, tile, offset, valid, gathered, around_ref, core_ref, *refs):
    table = dict(zip(LATTER, refs[: len(LATTER)]))
    out_ref, blocks, middle_ref, side_ref, surface_ref, sems = refs[len(LATTER) :]
    turn_id = pl.program_id(0)
    patch_count = out_ref.shape[0]
    each = around_ref.shape[0]
    per_row = gathered.shape[2] // LANES
    tiles = gathered.shape[0] * per_row
    lane = lax.broadcasted_iota(jnp.int32, (1, LANES), 1)
    halves = lane < LANES // 2
    half = SHIFTS // 2

    def place_of(k):
        place = owner[k] * per_row + tile[k] % per_row
        row = tile[k] // per_row * PATCH_SIDE + HALO - EDGE + offset[0, k]
        return place, row, jnp.minimum(row // 16 * 16, rows_total - ROWS)

    def fetch(turn, slot):
        made = []
        for n in range(each):
            place, _, base = place_of(turn * each + n)
            for c in range(3):
                block = jnp.minimum(jnp.maximum(place + c - 1, 0), tiles - 1)
                made.append(
                    pltpu.make_async_copy(
                        gathered.at[
                            block // per_row,
                            pl.ds(pl.multiple_of(base, 16), ROWS),
                            pl.ds(pl.multiple_of(block % per_row * LANES, LANES), LANES),
                        ],
                        blocks.at[slot, n, c],
                        sems.at[slot, n, c],
                    )
                )
        return made

    slot = turn_id % 2

    @pl.when(turn_id == 0)
    def _():
        for copy in fetch(0, 0):
            copy.start()

    @pl.when(turn_id + 1 < pl.num_programs(0))
    def _():
        for copy in fetch(turn_id + 1, 1 - slot):
            copy.start()

    for copy in fetch(turn_id, slot):
        copy.wait()

    inners, edges, found = [], [], []
    for n in range(each):
        k = turn_id * each + n
        place, row, base = place_of(k)
        right_end = jnp.where(place == tiles - 1, 0, LANES // 2)
        left_start = jnp.where(place == 0, LANES, LANES // 2)
        middle_ref[n] = blocks[slot, n, 1].astype(F32)
        side_ref[n] = jnp.where(
            lane < right_end,
            blocks[slot, n, 2].astype(F32),
            jnp.where(lane >= left_start, blocks[slot, n, 0].astype(F32), 0.0),
        )
        shown = pl.ds(row - base, SEARCH)
        dx = offset[1, k]
        turn = jnp.where(dx > 0, LANES - dx, -dx)
        centre = pltpu.roll(middle_ref[n, shown, :], turn, 1)
        side = pltpu.roll(side_ref[n, shown, :], turn, 1)
        within = (lane + dx >= 0) & (lane + dx < LANES)
        inner = jnp.where(within, centre, side)
        edge = jnp.where(within, side, centre).astype(BF16)
        mean, gain = statistics(inner[EDGE : EDGE + PATCH_SIDE])
        inners.append(inner.astype(BF16))
        edges.append(edge)
        found.append((mean, gain))

    lines = []
    for n, (line, rim) in enumerate(across(inners, edges, table, "search")):
        mean, gain = found[n]
        full, inside = spectra(line, rim, mean, table, "search", 1)
        inside = inside * gain[:, :1]
        a, b, c, d = [
            ahead + behind
            for ahead, behind in zip(matched(full, core_ref[n]), matched(inside, around_ref[n]))
        ]
        spectrum = jnp.concatenate(
            [jnp.concatenate([a, c], axis=1), jnp.concatenate([b, d], axis=1)], axis=0
        )
        scale = valid[turn_id * each + n].astype(F32) / (2.0 * PATCH_SIDE * CYCLE * CYCLE)
        lines.append(stacked(table["back_down"], spectrum) * scale)

    high, low = two(jnp.concatenate(lines, axis=0))
    surface = dot(jnp.concatenate([high, low, high], axis=1), table["back_across"][...])
    for n in range(each):
        k = turn_id * each + n
        even = surface[2 * n * half : (2 * n + 1) * half]
        odd = surface[(2 * n + 1) * half : (2 * n + 2) * half]
        surface_ref[pl.ds(pl.multiple_of(k * half, half), half), :] = jnp.where(halves, even, odd)

    @pl.when(turn_id == pl.num_programs(0) - 1)
    def _():
        for r in range(half):
            out_ref[:, r * LANES : (r + 1) * LANES] = surface_ref[
                pl.ds(r, patch_count, stride=half), :
            ]


def windows(owner, tile, offset, valid, gathered, around, core):
    patch_count = tile.shape[0]
    made = tables()
    latter = [jnp.asarray(made[name]) for name in LATTER]
    spectrum = around.shape
    dma = pltpu.SemaphoreType.DMA
    each = EACH
    block = pl.BlockSpec((each,) + spectrum[1:], lambda k, *_: (k, 0, 0))
    return pl.pallas_call(
        functools.partial(correlate, gathered.shape[1]),
        out_shape=jax.ShapeDtypeStruct((patch_count, SHIFTS * SHIFTS), F32),
        grid_spec=pltpu.PrefetchScalarGridSpec(
            num_scalar_prefetch=4,
            grid=(patch_count // each,),
            in_specs=[pl.BlockSpec(memory_space=pl.ANY), block, block]
            + [pl.BlockSpec(c.shape, lambda k, *_: (0, 0)) for c in latter],
            out_specs=pl.BlockSpec((patch_count, SHIFTS * SHIFTS), lambda k, *_: (0, 0)),
            scratch_shapes=[
                pltpu.VMEM((2, each, 3, ROWS, LANES), gathered.dtype),
                pltpu.VMEM((each, ROWS, LANES), F32),
                pltpu.VMEM((each, ROWS, LANES), F32),
                pltpu.VMEM((patch_count * SHIFTS // 2, LANES), F32),
                dma((2, each, 3)),
            ],
        ),
    )(owner, tile, offset, valid, gathered, around, core, *latter)


def on_device(bands, strips, first_scene, second_scene, owner_strip, target_tile, offsets, valid_mask):
    patch_count = target_tile.shape[-1]
    rows, cols = second_scene.shape
    made = tables()
    former = [jnp.asarray(made[name]) for name in FORMER]
    held = max(strips // 2, 1)
    dma = pltpu.SemaphoreType.DMA
    pieces = SPLIT + 2
    spectrum = (patch_count, 2 * BINS, WIDE)
    gathered, around, core = pl.pallas_call(
        functools.partial(exchange, bands, strips),
        out_shape=(
            jax.ShapeDtypeStruct((strips, rows + 2 * HALO, cols), second_scene.dtype),
            jax.ShapeDtypeStruct(spectrum, F32),
            jax.ShapeDtypeStruct(spectrum, F32),
        ),
        in_specs=[pl.BlockSpec(memory_space=pl.ANY)] * (2 + len(FORMER)),
        out_specs=[pl.BlockSpec(memory_space=pl.ANY)] * 3,
        scratch_shapes=[
            pltpu.VMEM((rows + 2 * EDGE, cols + 2 * LANES), first_scene.dtype),
            pltpu.VMEM(spectrum, F32),
            pltpu.VMEM(spectrum, F32),
            pltpu.VMEM((HALO, cols), second_scene.dtype),
            *[pltpu.VMEM(c.shape, c.dtype) for c in former],
            dma((8,)),
            dma((8,)),
            dma((held, pieces)),
            dma((held, pieces)),
            dma((held, 2)),
            dma((held, 2)),
            dma((held, pieces)),
            dma((held, pieces)),
            dma((held, 2)),
            dma((held, 2)),
            dma((2,)),
            dma((len(FORMER),)),
            dma((2, patch_count)),
            dma((strips, 2)),
        ],
        compiler_params=pltpu.CompilerParams(collective_id=0, has_side_effects=True),
    )(first_scene, second_scene, *former)
    result = windows(
        owner_strip.reshape(patch_count),
        target_tile.reshape(patch_count),
        offsets.reshape(patch_count, 2).T,
        valid_mask.reshape(patch_count),
        gathered,
        around,
        core,
    )
    return result.reshape(1, 1, patch_count, SHIFTS * SHIFTS)


def solution(mesh):
    return jax.shard_map(
        functools.partial(on_device, mesh.shape["band"], mesh.shape["strip"]),
        mesh=mesh,
        in_specs=(
            P("band", "strip"),
            P("band", "strip"),
            P("band", "strip", None, None),
            P("band", "strip", None),
            P("band", "strip", None, None),
            P("band", "strip", None),
        ),
        out_specs=P("band", "strip", None, None),
        check_vma=False,
    )
```
